32 devices in a mesh: dp: 8 (over z, x), tensor: 4 (over y, core).
Axes of the slice: x: 2, y: 2, z: 4, core: 2. Of those that a mesh axis runs over, the one named last changes fastest.
Arguments:
- tokens: bfloat16 [3072, 2048], P('dp', 'tensor'), may hold values from -6 to 6
- partner_bits: int32 [4, 2], replicated, may hold values from 0 to 1, as said below
- w_up: bfloat16 [4, 3, 512, 1024], P('tensor', None, 'dp'), may hold values from -0.15625 to 0.15625
- w_down: bfloat16 [4, 3, 1024, 512], P('tensor', None, 'dp'), may hold values from -0.109375 to 0.109375
Outputs:
- mixed: bfloat16 [3072, 2048], P('dp', 'tensor')
The draws below stay inside these ranges and needn't reach their ends.
Inputs may be any that keep to these rules, and one draw needn't show every extreme that they name: Each row of partner_bits lists each of 0 to 1 exactly once.
All inputs are finite; a program needn't handle non-finite values.
Results may differ from the reference program's by a relative error of at most 0.0057.
Values may be sent and summed in bfloat16 or wider, within the bound.
A program may use at most 64 MiB of HBM per device.

```python
import jax
import jax.numpy as jnp
from jax import lax

D_BLK = 512
FF_BLK = 1024
NB = 4
LINKS = 2
D = 2048
TOKENS = 3072


def draw_partner_bits(key, part):
    scores = jax.random.randint(key, (NB, LINKS), 0, 1 << 20) * LINKS + jnp.arange(LINKS, dtype=jnp.int32)[None, :]
    return jnp.argsort(scores, axis=1).astype(jnp.int32)


def shard_levels(own_key, extent, cuts, smallest, largest):
    def one(axis_at, blocks):
        steps = jax.random.uniform(jax.random.fold_in(jax.random.fold_in(own_key, 6), axis_at), (blocks,), jnp.float32, smallest / len(cuts), largest / len(cuts))
        return jnp.repeat(jnp.exp(steps), extent[axis_at] // blocks).reshape((-1,) + (1,) * (len(extent) - axis_at - 1))

    loudness = one(*cuts[0])
    for cut in cuts[1:]:
        loudness = loudness * one(*cut)
    return loudness


def bell_draw(own_key, extent, spread, bound, split=(), kind=jnp.bfloat16):
    values = spread * jax.random.normal(own_key, extent, jnp.float32)
    if split:
        values = values * shard_levels(own_key, extent, split, -0.22, 0.18)
    return jnp.clip(values, -bound, bound).astype(kind)


def setup_inputs(seed: int = 0) -> dict:
    key_of = jax.random.split(jax.random.key(seed), 5)
    return {
        "tokens": bell_draw(key_of[0], (TOKENS, D), 1.0, 6.0, ((0, 8), (1, 4))),
        "partner_bits": draw_partner_bits(jax.random.fold_in(key_of[4], 71), 0),
        "w_up": bell_draw(key_of[2], (NB, LINKS + 1, D_BLK, FF_BLK), ((LINKS + 1) * D_BLK) ** -0.5, 0.15625, ((0, 4), (2, 8))),
        "w_down": bell_draw(key_of[3], (NB, LINKS + 1, FF_BLK, D_BLK), ((LINKS + 1) * FF_BLK) ** -0.5, 0.109375, ((0, 4), (2, 8))),
    }


def reference(tokens, partner_bits, w_up, w_down):
    blocks = tokens.reshape(TOKENS, NB, D_BLK)
    rows = jnp.arange(NB, dtype=jnp.int32)
    shifted = jnp.left_shift(jnp.ones_like(partner_bits), partner_bits)
    link = jnp.concatenate([rows[:, None], jnp.bitwise_xor(rows[:, None], shifted)], axis=1).astype(jnp.int32)

    def one_block(total, j):
        sel = link[j]
        inputs = jnp.take(blocks, sel, axis=1).astype(jnp.float32)
        up_w = w_up[j].astype(jnp.float32)
        pre = jnp.einsum("tsd,sdf->tf", inputs, up_w, precision=lax.Precision.HIGHEST)
        hidden = jax.nn.gelu(pre, approximate=True).astype(jnp.bfloat16)
        down_w = w_down[j].astype(jnp.float32)
        terms = jnp.einsum("tf,sfd->std", hidden.astype(jnp.float32), down_w, precision=lax.Precision.HIGHEST)
        terms = terms.astype(jnp.bfloat16).astype(jnp.float32)
        total = total.at[sel].add(terms)
        return total, None

    start = jnp.zeros((NB, TOKENS, D_BLK), jnp.float32)
    total, unused = lax.scan(one_block, start, jnp.arange(NB, dtype=jnp.int32))
    return jnp.transpose(total, (1, 0, 2)).reshape(TOKENS, D).astype(jnp.bfloat16)
```

```python
import functools

import jax
import jax.numpy as jnp
from jax import lax
from jax.experimental import pallas as pl
from jax.experimental.pallas import tpu as pltpu
from jax.sharding import PartitionSpec as P

MESH = pl.DeviceIdType.MESH
LANES = 128
TOKEN_PIECES = 3
SUM_PIECES = 2


def flip(index, mask):
    bit = 1
    while bit <= mask:
        if mask & bit:
            index = index + (1 - 2 * ((index // bit) % 2)) * bit
        bit *= 2
    return index


def when(condition, body):
    if isinstance(condition, bool):
        if condition:
            body()
    else:
        pl.when(condition)(body)


def kernel(
    nz, planes, bits_ref, tok_ref, up_raw, down_raw, out_ref,
    tok, up, down, hid, stage, landed, own, down_in, down_mine, down_away,
    local_sem, near_send, near_recv, pair_send, pair_recv, far_send, far_recv,
    up_send, up_recv, up_side_send, up_side_recv, slice_send, slice_recv,
    down_send, down_recv, down_side_send, down_side_recv,
    hid_send, hid_recv, sum_send, sum_recv,
):
    slots, rows, width = tok.shape[0], tok.shape[2], tok.shape[3]
    rows_up, rows_down = up_raw.shape[2], down_raw.shape[2]
    group = planes * 2 * rows_down
    groups = nz // (2 * planes)
    me, rank = lax.axis_index("dp"), lax.axis_index("tensor")
    z, x = me // 2, me % 2
    other = z * 2 + (1 - x)
    partner = [rank] + [flip(rank, 1 << bit) for bit in range(slots - 1)]
    others = [mask for mask in range(2, nz)] + [1]

    def plane(mask):
        return flip(z, mask) * 2 + x

    def remote(src, dst, send, recv, device):
        return pltpu.make_async_remote_copy(
            src_ref=src, dst_ref=dst, send_sem=send, recv_sem=recv,
            device_id=device, device_id_type=MESH,
        )

    def up_rows(at_z, at_x):
        return pl.ds(pl.multiple_of((at_z * 2 + at_x) * rows_up, rows_up), rows_up)

    def up_place(mask, at_x, c):
        return up.at[:, up_rows(flip(z, mask), at_x), c * group:(c + 1) * group]

    def up_source(mask, c):
        parity = (z + mask) % 2
        first = pl.multiple_of((2 * c + parity) * group, group)
        return up_raw.at[0, :, :, pl.ds(first, group)]

    def down_rows(at_z, at_x):
        row = (at_z // (2 * planes)) * group + ((at_z % planes) * 2 + at_x) * rows_down
        return pl.ds(pl.multiple_of(row, rows_down), rows_down)

    def gives_down(mask):
        if planes == 1:
            return mask % 2 == 0
        return (z + mask) % 2 == (z // planes) % 2

    def takes_down(mask):
        if planes == 1:
            return mask % 2 == 0
        return z % 2 == (flip(z, mask) // planes) % 2

    def down_source(slot):
        return down_raw.at[0, 0] if slot == 0 else down_mine.at[slot]

    piece = rows // TOKEN_PIECES
    cut = width // SUM_PIECES

    def near_copy(slot):
        return remote(tok_ref, tok.at[slot, 0], near_send.at[slot], near_recv.at[slot], (me, partner[slot]))

    def pair_copy(i):
        part = pl.ds(i * piece, piece)
        return remote(tok_ref.at[part], tok.at[0, 1, part], pair_send.at[i], pair_recv.at[i], (plane(1), rank))

    def far_copy(slot, i):
        part = pl.ds(i * piece, piece)
        return remote(
            tok.at[0, 1, part], tok.at[slot, 1, part], far_send.at[slot, i], far_recv.at[slot, i], (me, partner[slot])
        )

    def up_copy(mask, c):
        return remote(
            up_source(mask, c), up_place(0, x, c), up_send.at[c, mask], up_recv.at[c, mask], (plane(mask), rank)
        )

    def up_side(mask, c):
        src = up_source(0, c) if mask == 0 else up_place(mask, x, c)
        return remote(
            src, up_place(mask, x, c), up_side_send.at[c, mask], up_side_recv.at[c, mask], (other, rank)
        )

    def slice_copy(slot):
        return remote(
            down_away.at[slot - 1], down_mine.at[slot], slice_send.at[slot], slice_recv.at[slot], (me, partner[slot])
        )

    def down_copy(mask, slot):
        return remote(
            down_source(slot), down.at[slot, down_rows(z, x)],
            down_send.at[mask, slot], down_recv.at[mask, slot], (plane(mask), rank),
        )

    def down_side(mask, slot):
        place = down.at[slot, down_rows(flip(z, mask), x)]
        return remote(
            down_source(slot) if mask == 0 else place, place,
            down_side_send.at[mask, slot], down_side_recv.at[mask, slot], (other, rank),
        )

    def down_local(slot):
        return pltpu.make_async_copy(down_source(slot), down.at[slot, down_rows(z, x)], local_sem.at[2 + slot])

    def hid_copy(slot, c, far):
        columns = pl.ds(c * group, group)
        return remote(
            hid.at[0, far, :, columns], hid.at[slot, far, :, columns],
            hid_send.at[slot, c, far], hid_recv.at[slot, c, far], (me, partner[slot]),
        )

    def sum_copy(i):
        columns = pl.ds(i * cut, cut)
        return remote(stage.at[:, columns], landed.at[:, columns], sum_send.at[i], sum_recv.at[i], (plane(1), rank))

    def up_local(c):
        return pltpu.make_async_copy(up_source(0, c), up_place(0, x, c), local_sem.at[2 + slots + c])

    far_slots = range(slots - 1, 0, -1)

    fetch_down = pltpu.make_async_copy(down_raw.at[0], down_in, local_sem.at[0])
    fetch_tok = pltpu.make_async_copy(tok_ref, tok.at[0, 0], local_sem.at[1])
    fetch_down.start()
    fetch_tok.start()
    for c in range(groups):
        up_local(c).start()
    barrier = pltpu.get_barrier_semaphore()
    greeted = [(plane(mask), rank) for mask in range(1, nz)] + [(other, rank)]
    greeted += [(me, partner[slot]) for slot in range(1, slots)]
    for device in greeted:
        pl.semaphore_signal(barrier, inc=1, device_id=device, device_id_type=MESH)
    bits = [jnp.clip(bits_ref[slot, rank], 0, slots - 2) for slot in range(slots - 1)]
    pl.semaphore_wait(barrier, len(greeted))

    for i in range(TOKEN_PIECES):
        pair_copy(i).start()
    for slot in far_slots:
        near_copy(slot).start()
    up_side(0, 0).start()
    for c in range(groups):
        for mask in others:
            up_copy(mask, c).start()
    for c in range(1, groups):
        up_side(0, c).start()
    fetch_down.wait()
    for bit in range(slots - 1):
        pick = jnp.int32(0)
        for slot in range(slots - 1):
            pick += jnp.where(bits[slot] == bit, slot + 1, 0)
        down_away[bit] = down_in[jnp.minimum(pick, slots - 1)]
    for slot in far_slots:
        slice_copy(slot).start()

    def spread_down(slot):
        for mask in others:
            when(gives_down(mask), lambda: down_copy(mask, slot).start())

        def keep():
            down_side(0, slot).start()
            down_local(slot).start()

        when(takes_down(0), keep)

    spread_down(0)

    def token_piece(i):
        pair_copy(i).wait_recv()
        for slot in far_slots:
            far_copy(slot, i).start()

    def up_arrived(mask, c):
        up_copy_from = remote(
            up_source(mask, c), up_place(mask, x, c), up_send.at[c, mask], up_recv.at[c, mask], (plane(mask), rank)
        )
        up_copy_from.wait_recv()
        up_side(mask, c).start()

    def down_arrived(mask, slot):
        def body():
            place = down.at[slot, down_rows(flip(z, mask), x)]
            remote(
                place, place, down_send.at[mask, slot], down_recv.at[mask, slot], (plane(mask), rank)
            ).wait_recv()
            down_side(mask, slot).start()

        when(takes_down(mask), body)

    def up_complete(c):
        up_local(c).wait()
        for mask in range(nz):
            place = up_place(mask, 1 - x, c)
            remote(place, place, up_side_send.at[c, mask], up_side_recv.at[c, mask], (other, rank)).wait_recv()

    def hidden(c):
        columns = slice(c * group, (c + 1) * group)
        for far in (1, 0):
            pre = jnp.dot(tok[0, far], up[0, :, columns], preferred_element_type=jnp.float32)
            for slot in range(1, slots):
                pre += jnp.dot(
                    tok[1 + bits[slot - 1], far], up[slot, :, columns], preferred_element_type=jnp.float32
                )
            hid[0, far, :, columns] = jax.nn.gelu(pre, approximate=True).astype(hid.dtype)
            for slot in far_slots:
                hid_copy(slot, c, far).start()

    steps = max(TOKEN_PIECES, len(others))
    for step in range(steps):
        if step < TOKEN_PIECES:
            token_piece(step)
        if step < len(others):
            up_arrived(others[step], 0)
    for slot in range(1, slots):
        slice_copy(slot).wait_recv()
        spread_down(slot)
    fetch_tok.wait()
    for slot in far_slots:
        near_copy(slot).wait_recv()
        for i in range(TOKEN_PIECES):
            far_copy(slot, i).wait_recv()
    for c in range(groups):
        up_complete(c)
        hidden(c)
        if c + 1 < groups:
            for mask in others:
                up_arrived(mask, c + 1)
    for slot in range(slots):
        for mask in others:
            down_arrived(mask, slot)
    for slot in range(slots):
        for mask in range(nz):
            def body():
                if mask == 0:
                    down_local(slot).wait()
                place = down.at[slot, down_rows(flip(z, mask), 1 - x)]
                remote(
                    place, place, down_side_send.at[mask, slot], down_side_recv.at[mask, slot], (other, rank)
                ).wait_recv()

            when(takes_down(mask), body)

    def product(far, columns):
        total = jnp.dot(hid[0, far], down[0, :, columns], preferred_element_type=jnp.float32)
        for slot in range(1, slots):
            total += jnp.dot(hid[slot, far], down[slot, :, columns], preferred_element_type=jnp.float32)
        return total

    for c in range(groups):
        for slot in far_slots:
            hid_copy(slot, c, 1).wait_recv()
    for i in range(SUM_PIECES):
        columns = slice(i * cut, (i + 1) * cut)
        stage[:, columns] = product(1, columns).astype(stage.dtype)
        sum_copy(i).start()
    for c in range(groups):
        for slot in far_slots:
            hid_copy(slot, c, 0).wait_recv()
    own[...] = product(0, slice(None))
    for i in range(SUM_PIECES):
        sum_copy(i).wait_recv()
        columns = slice(i * cut, (i + 1) * cut)
        out_ref[:, columns] = (own[:, columns] + landed[:, columns].astype(jnp.float32)).astype(out_ref.dtype)

    for i in range(TOKEN_PIECES):
        pair_copy(i).wait_send()
    for slot in far_slots:
        near_copy(slot).wait_send()
        slice_copy(slot).wait_send()
        for i in range(TOKEN_PIECES):
            far_copy(slot, i).wait_send()
        for c in range(groups):
            for far in (1, 0):
                hid_copy(slot, c, far).wait_send()
    for c in range(groups):
        for mask in range(nz):
            if mask:
                up_copy(mask, c).wait_send()
            up_side(mask, c).wait_send()
    for slot in range(slots):
        for mask in range(nz):
            if mask:
                when(gives_down(mask), lambda: down_copy(mask, slot).wait_send())
            when(takes_down(mask), lambda: down_side(mask, slot).wait_send())
    for i in range(SUM_PIECES):
        sum_copy(i).wait_send()


def on_device(tokens, partner_bits, w_up, w_down):
    nz = lax.axis_size("dp") // 2
    slots = w_up.shape[1]
    rows, width = tokens.shape
    hidden = w_up.shape[3]
    rows_down = w_down.shape[2]
    half = hidden // 2
    planes = max(1, LANES // (2 * rows_down))
    groups = nz // (2 * planes)
    kind = tokens.dtype
    dma = pltpu.SemaphoreType.DMA
    return pl.pallas_call(
        functools.partial(kernel, nz, planes),
        out_shape=jax.ShapeDtypeStruct((rows, width), kind),
        in_specs=[pl.BlockSpec(memory_space=pltpu.SMEM)] + [pl.BlockSpec(memory_space=pl.ANY)] * 3,
        out_specs=pl.BlockSpec(memory_space=pltpu.VMEM),
        scratch_shapes=[
            pltpu.VMEM((slots, 2, rows, width), kind),
            pltpu.VMEM((slots, width, half), kind),
            pltpu.VMEM((slots, half, width), kind),
            pltpu.VMEM((slots, 2, rows, half), kind),
            pltpu.VMEM((rows, width), kind),
            pltpu.VMEM((rows, width), kind),
            pltpu.VMEM((rows, width), jnp.float32),
            pltpu.VMEM(w_down.shape[1:], kind),
            pltpu.VMEM(w_down.shape[1:], kind),
            pltpu.VMEM((slots - 1,) + w_down.shape[2:], kind),
            dma((2 + slots + groups,)),
            dma((slots,)),
            dma((slots,)),
            dma((TOKEN_PIECES,)),
            dma((TOKEN_PIECES,)),
            dma((slots, TOKEN_PIECES)),
            dma((slots, TOKEN_PIECES)),
            dma((groups, nz)),
            dma((groups, nz)),
            dma((groups, nz)),
            dma((groups, nz)),
            dma((slots,)),
            dma((slots,)),
            dma((nz, slots)),
            dma((nz, slots)),
            dma((nz, slots)),
            dma((nz, slots)),
            dma((slots, groups, 2)),
            dma((slots, groups, 2)),
            dma((SUM_PIECES,)),
            dma((SUM_PIECES,)),
        ],
        compiler_params=pltpu.CompilerParams(
            collective_id=0, has_side_effects=True, vmem_limit_bytes=67043328
        ),
    )(partner_bits.T, tokens, w_up, w_down)


def solution(mesh):
    in_specs = (
        P("dp", "tensor"),
        P(),
        P("tensor", None, "dp", None),
        P("tensor", None, "dp", None),
    )
    return jax.shard_map(
        on_device, mesh=mesh, in_specs=in_specs, out_specs=P("dp", "tensor"), check_vma=False
    )
```

```python
import functools

import jax
import jax.numpy as jnp
from jax import lax
from jax.experimental import pallas as pl
from jax.experimental.pallas import tpu as pltpu
from jax.sharding import PartitionSpec as P

MESH = pl.DeviceIdType.MESH
LANES = 128
TOKEN_PIECES = 3
ROW_PIECES = 2
LATE_DOWN = True
ORDER = (
    "far0", "slices", "keep", "tokens", "close0", "spread", "far1", "ready",
    "hidden0", "close1", "hidden1", "down0", "near",
)
DOWN_SHARES = (2, 4, 4)


def flip(index, mask):
    bit = 1
    while bit <= mask:
        if mask & bit:
            index = index + (1 - 2 * ((index // bit) % 2)) * bit
        bit *= 2
    return index


def column_pieces(width):
    pieces, first = [], 0
    for share in DOWN_SHARES:
        pieces.append((first, width // share))
        first += width // share
    return pieces


def when(condition, body):
    if isinstance(condition, bool):
        if condition:
            body()
    else:
        pl.when(condition)(body)


def kernel(
    nz, planes, bits_ref, tok_ref, up_raw, down_raw, out_ref,
    tok, up, down, hid, stage, landed, own, down_in, down_mine, down_away,
    local_sem, near_send, near_recv, pair_send, pair_recv, far_send, far_recv,
    up_send, up_recv, up_side_send, up_side_recv, slice_send, slice_recv,
    down_send, down_recv, down_side_send, down_side_recv,
    hid_send, hid_recv, sum_send, sum_recv,
):
    slots, rows, width = tok.shape[0], tok.shape[2], tok.shape[3]
    rows_up, rows_down = up_raw.shape[2], down_raw.shape[2]
    group = planes * 2 * rows_down
    groups = nz // (2 * planes)
    me, rank = lax.axis_index("dp"), lax.axis_index("tensor")
    z, x = me // 2, me % 2
    other = z * 2 + (1 - x)
    partner = [rank] + [flip(rank, 1 << bit) for bit in range(slots - 1)]
    others = [mask for mask in range(2, nz)] + [1]

    def plane(mask):
        return flip(z, mask) * 2 + x

    def remote(src, dst, send, recv, device):
        return pltpu.make_async_remote_copy(
            src_ref=src, dst_ref=dst, send_sem=send, recv_sem=recv,
            device_id=device, device_id_type=MESH,
        )

    def up_rows(at_z, at_x):
        return pl.ds(pl.multiple_of((at_z * 2 + at_x) * rows_up, rows_up), rows_up)

    def up_place(mask, at_x, c):
        return up.at[:, up_rows(flip(z, mask), at_x), c * group:(c + 1) * group]

    def up_source(mask, c):
        parity = (z + mask) % 2
        first = pl.multiple_of((2 * c + parity) * group, group)
        return up_raw.at[0, :, :, pl.ds(first, group)]

    def down_rows(at_z, at_x):
        row = (at_z // (2 * planes)) * group + ((at_z % planes) * 2 + at_x) * rows_down
        return pl.ds(pl.multiple_of(row, rows_down), rows_down)

    def gives_down(mask):
        if planes == 1:
            return mask % 2 == 0
        return (z + mask) % 2 == (z // planes) % 2

    def takes_down(mask):
        if planes == 1:
            return mask % 2 == 0
        return z % 2 == (flip(z, mask) // planes) % 2

    piece = rows // TOKEN_PIECES
    cut = rows // ROW_PIECES
    pieces = column_pieces(width)

    def near_copy(slot):
        return remote(tok_ref, tok.at[slot, 0], near_send.at[slot], near_recv.at[slot], (me, partner[slot]))

    def pair_copy(i):
        part = pl.ds(i * piece, piece)
        return remote(tok_ref.at[part], tok.at[0, 1, part], pair_send.at[i], pair_recv.at[i], (plane(1), rank))

    def far_copy(slot, i):
        part = pl.ds(i * piece, piece)
        return remote(
            tok.at[0, 1, part], tok.at[slot, 1, part], far_send.at[slot, i], far_recv.at[slot, i], (me, partner[slot])
        )

    def up_copy(mask, c):
        return remote(
            up_source(mask, c), up_place(0, x, c), up_send.at[c, mask], up_recv.at[c, mask], (plane(mask), rank)
        )

    def up_side(mask, c):
        src = up_source(0, c) if mask == 0 else up_place(mask, x, c)
        return remote(
            src, up_place(mask, x, c), up_side_send.at[c, mask], up_side_recv.at[c, mask], (other, rank)
        )

    def slice_copy(slot):
        return remote(
            down_away.at[slot - 1], down_mine.at[slot], slice_send.at[slot], slice_recv.at[slot], (me, partner[slot])
        )

    def down_place(mask, at_x, q):
        first, wide = pieces[q]
        return down.at[:, down_rows(flip(z, mask), at_x), first:first + wide]

    def down_source(q):
        first, wide = pieces[q]
        return down_mine.at[:, :, first:first + wide]

    def down_copy(mask, q):
        return remote(
            down_source(q), down_place(0, x, q), down_send.at[mask, q], down_recv.at[mask, q], (plane(mask), rank)
        )

    def down_side(mask, q):
        src = down_source(q) if mask == 0 else down_place(mask, x, q)
        return remote(
            src, down_place(mask, x, q), down_side_send.at[mask, q], down_side_recv.at[mask, q], (other, rank)
        )

    def down_local(q):
        return pltpu.make_async_copy(down_source(q), down_place(0, x, q), local_sem.at[2 + q])

    def hid_copy(slot, c, far, i):
        part, columns = pl.ds(i * cut, cut), pl.ds(c * group, group)
        return remote(
            hid.at[0, far, part, columns], hid.at[slot, far, part, columns],
            hid_send.at[slot, c, far, i], hid_recv.at[slot, c, far, i], (me, partner[slot]),
        )

    def sum_copy(q):
        first, wide = pieces[q]
        columns = pl.ds(first, wide)
        return remote(stage.at[:, columns], landed.at[:, columns], sum_send.at[q], sum_recv.at[q], (plane(1), rank))


    def up_local(c):
        return pltpu.make_async_copy(up_source(0, c), up_place(0, x, c), local_sem.at[2 + len(pieces) + c])

    far_slots = range(slots - 1, 0, -1)

    fetch_down = pltpu.make_async_copy(down_raw.at[0], down_in, local_sem.at[0])
    fetch_tok = pltpu.make_async_copy(tok_ref, tok.at[0, 0], local_sem.at[1])
    fetch_down.start()
    fetch_tok.start()
    for c in range(groups):
        up_local(c).start()
    barrier = pltpu.get_barrier_semaphore()
    greeted = [(plane(mask), rank) for mask in range(1, nz)] + [(other, rank)]
    greeted += [(me, partner[slot]) for slot in range(1, slots)]
    for device in greeted:
        pl.semaphore_signal(barrier, inc=1, device_id=device, device_id_type=MESH)
    bits = [jnp.clip(bits_ref[slot, rank], 0, slots - 2) for slot in range(slots - 1)]
    fetch_down.wait()
    for bit in range(slots - 1):
        pick = jnp.int32(0)
        for slot in range(slots - 1):
            pick += jnp.where(bits[slot] == bit, slot + 1, 0)
        down_away[bit] = down_in[jnp.minimum(pick, slots - 1)]
    down_mine[0] = down_in[0]
    pl.semaphore_wait(barrier, len(greeted))

    def spread_down(q):
        for mask in others:
            when(gives_down(mask), lambda: down_copy(mask, q).start())

    def keep_down(q):
        def body():
            down_side(0, q).start()
            down_local(q).start()

        when(takes_down(0), body)

    def send_up(c, masks):
        for mask in masks:
            up_copy(mask, c).start()

    for slot in far_slots:
        slice_copy(slot).start()
    for slot in far_slots:
        near_copy(slot).start()
    send_up(0, others[:-1])
    for i in range(TOKEN_PIECES):
        pair_copy(i).start()
    send_up(0, others[-1:])
    up_side(0, 0).start()
    for c in range(1, groups):
        send_up(c, others)
        up_side(0, c).start()

    def token_piece(i):
        pair_copy(i).wait_recv()
        for slot in far_slots:
            far_copy(slot, i).start()

    def up_arrived(mask, c):
        up_copy_from = remote(
            up_source(mask, c), up_place(mask, x, c), up_send.at[c, mask], up_recv.at[c, mask], (plane(mask), rank)
        )
        up_copy_from.wait_recv()
        up_side(mask, c).start()

    def down_arrived(q):
        for mask in others:
            def body():
                place = down_place(mask, x, q)
                remote(
                    place, place, down_send.at[mask, q], down_recv.at[mask, q], (plane(mask), rank)
                ).wait_recv()
                down_side(mask, q).start()

            when(takes_down(mask), body)

    def down_complete(q):
        for mask in range(nz):
            def body():
                if mask == 0:
                    down_local(q).wait()
                place = down_place(mask, 1 - x, q)
                remote(
                    place, place, down_side_send.at[mask, q], down_side_recv.at[mask, q], (other, rank)
                ).wait_recv()

            when(takes_down(mask), body)

    def up_complete(c):
        up_local(c).wait()
        for mask in range(nz):
            place = up_place(mask, 1 - x, c)
            remote(place, place, up_side_send.at[c, mask], up_side_recv.at[c, mask], (other, rank)).wait_recv()

    def hidden(c, far):
        columns = slice(c * group, (c + 1) * group)
        for i in range(ROW_PIECES):
            part = slice(i * cut, (i + 1) * cut)
            pre = jnp.dot(tok[0, far, part], up[0, :, columns], preferred_element_type=jnp.float32)
            for slot in range(1, slots):
                pre += jnp.dot(
                    tok[1 + bits[slot - 1], far, part], up[slot, :, columns], preferred_element_type=jnp.float32
                )
            hid[0, far, part, columns] = jax.nn.gelu(pre, approximate=True).astype(hid.dtype)
            for slot in far_slots:
                hid_copy(slot, c, far, i).start()

    def slices_ready():
        for slot in range(1, slots):
            slice_copy(slot).wait_recv()

    def tokens_ready():
        fetch_tok.wait()
        for slot in far_slots:
            near_copy(slot).wait_recv()
            for i in range(TOKEN_PIECES):
                far_copy(slot, i).wait_recv()

    def distant_up(chunks):
        for c in chunks:
            for mask in others[:-1]:
                up_arrived(mask, c)

    def close_up(chunks):
        for c in chunks:
            for mask in others[-1:]:
                up_arrived(mask, c)

    def up_hidden(chunks, far):
        for c in chunks:
            if far:
                up_complete(c)
            hidden(c, far)

    begin, later = range(1), range(1, groups)
    steps = {
        "far0": lambda: distant_up(begin),
        "far1": lambda: distant_up(later),
        "close0": lambda: close_up(begin),
        "close1": lambda: close_up(later),
        "slices": slices_ready,
        "spread": lambda: [spread_down(q) for q in range(len(pieces))],
        "keep": lambda: [keep_down(q) for q in range(len(pieces))],
        "tokens": lambda: [token_piece(i) for i in range(TOKEN_PIECES)],
        "ready": tokens_ready,
        "hidden0": lambda: up_hidden(begin, 1),
        "hidden1": lambda: up_hidden(later, 1),
        "near": lambda: up_hidden(range(groups), 0),
        "near0": lambda: up_hidden(begin, 0),
        "near1": lambda: up_hidden(later, 0),
        "down0": lambda: down_arrived(0),
        "down1": lambda: down_arrived(1),
        "down2": lambda: down_arrived(2),
    }
    for step in ORDER:
        steps[step]()

    def product(far, part, columns):
        total = jnp.dot(hid[0, far, part], down[0, :, columns], preferred_element_type=jnp.float32)
        for slot in range(1, slots):
            total += jnp.dot(hid[slot, far, part], down[slot, :, columns], preferred_element_type=jnp.float32)
        return total

    def hid_arrived(far, i):
        for c in range(groups):
            for slot in far_slots:
                hid_copy(slot, c, far, i).wait_recv()

    for q, (first, wide) in enumerate(pieces):
        columns = slice(first, first + wide)
        if q == 0 and LATE_DOWN:
            down_arrived(1)
        if q == 1 and LATE_DOWN:
            down_arrived(2)
        down_complete(q)
        for i in range(ROW_PIECES):
            part = slice(i * cut, (i + 1) * cut)
            if q == 0:
                hid_arrived(1, i)
            stage[part, columns] = product(1, part, columns).astype(stage.dtype)
        sum_copy(q).start()
    for i in range(ROW_PIECES):
        part = slice(i * cut, (i + 1) * cut)
        hid_arrived(0, i)
        own[part] = product(0, part, slice(None))
    for q, (first, wide) in enumerate(pieces):
        columns = slice(first, first + wide)
        sum_copy(q).wait_recv()
        out_ref[:, columns] = (own[:, columns] + landed[:, columns].astype(jnp.float32)).astype(out_ref.dtype)

    for i in range(TOKEN_PIECES):
        pair_copy(i).wait_send()
    for slot in far_slots:
        near_copy(slot).wait_send()
        slice_copy(slot).wait_send()
        for i in range(TOKEN_PIECES):
            far_copy(slot, i).wait_send()
        for c in range(groups):
            for far in (1, 0):
                for i in range(ROW_PIECES):
                    hid_copy(slot, c, far, i).wait_send()
    for c in range(groups):
        for mask in range(nz):
            if mask:
                up_copy(mask, c).wait_send()
            up_side(mask, c).wait_send()
    for q in range(len(pieces)):
        for mask in range(nz):
            if mask:
                when(gives_down(mask), lambda: down_copy(mask, q).wait_send())
            when(takes_down(mask), lambda: down_side(mask, q).wait_send())
        sum_copy(q).wait_send()


def on_device(tokens, partner_bits, w_up, w_down):
    nz = lax.axis_size("dp") // 2
    slots = w_up.shape[1]
    rows, width = tokens.shape
    hidden = w_up.shape[3]
    rows_down = w_down.shape[2]
    half = hidden // 2
    planes = max(1, LANES // (2 * rows_down))
    groups = nz // (2 * planes)
    count = len(DOWN_SHARES)
    kind = tokens.dtype
    dma = pltpu.SemaphoreType.DMA
    return pl.pallas_call(
        functools.partial(kernel, nz, planes),
        out_shape=jax.ShapeDtypeStruct((rows, width), kind),
        in_specs=[pl.BlockSpec(memory_space=pltpu.SMEM)] + [pl.BlockSpec(memory_space=pl.ANY)] * 3,
        out_specs=pl.BlockSpec(memory_space=pltpu.VMEM),
        scratch_shapes=[
            pltpu.VMEM((slots, 2, rows, width), kind),
            pltpu.VMEM((slots, width, half), kind),
            pltpu.VMEM((slots, half, width), kind),
            pltpu.VMEM((slots, 2, rows, half), kind),
            pltpu.VMEM((rows, width), kind),
            pltpu.VMEM((rows, width), kind),
            pltpu.VMEM((rows, width), jnp.float32),
            pltpu.VMEM(w_down.shape[1:], kind),
            pltpu.VMEM(w_down.shape[1:], kind),
            pltpu.VMEM((slots - 1,) + w_down.shape[2:], kind),
            dma((2 + count + groups,)),
            dma((slots,)),
            dma((slots,)),
            dma((TOKEN_PIECES,)),
            dma((TOKEN_PIECES,)),
            dma((slots, TOKEN_PIECES)),
            dma((slots, TOKEN_PIECES)),
            dma((groups, nz)),
            dma((groups, nz)),
            dma((groups, nz)),
            dma((groups, nz)),
            dma((slots,)),
            dma((slots,)),
            dma((nz, count)),
            dma((nz, count)),
            dma((nz, count)),
            dma((nz, count)),
            dma((slots, groups, 2, ROW_PIECES)),
            dma((slots, groups, 2, ROW_PIECES)),
            dma((count,)),
            dma((count,)),
        ],
        compiler_params=pltpu.CompilerParams(
            collective_id=0, has_side_effects=True, vmem_limit_bytes=67043328
        ),
    )(partner_bits.T, tokens, w_up, w_down)


def solution(mesh):
    in_specs = (
        P("dp", "tensor"),
        P(),
        P("tensor", None, "dp", None),
        P("tensor", None, "dp", None),
    )
    return jax.shard_map(
        on_device, mesh=mesh, in_specs=in_specs, out_specs=P("dp", "tensor"), check_vma=False
    )
```

```python
import functools

import jax
import jax.numpy as jnp
from jax import lax
from jax.experimental import pallas as pl
from jax.experimental.pallas import tpu as pltpu
from jax.sharding import PartitionSpec as P

MESH = pl.DeviceIdType.MESH
LANES = 128
VMEM_BYTES = 65273856
TOKEN_PIECES = 1
ROW_PIECES = 2
LATE_DOWN = True
ORDER = ("slices", "keep", "spreadE", "far0", "tokens", "spreadM", "mixed", "ready", "hidden0", "close1", "hidden1", "down0", "near")
DOWN_SHARES = (2, 4, 4)


def flip(index, mask):
    bit = 1
    while bit <= mask:
        if mask & bit:
            index = index + (1 - 2 * ((index // bit) % 2)) * bit
        bit *= 2
    return index


def column_pieces(width):
    pieces, first = [], 0
    for share in DOWN_SHARES:
        pieces.append((first, width // share))
        first += width // share
    return pieces


def when(condition, body):
    if isinstance(condition, bool):
        if condition:
            body()
    else:
        pl.when(condition)(body)


def kernel(
    nz, planes, bits_ref, tok_ref, up_raw, down_raw, own_ref, landed,
    tok, up, down, hid, stage, down_in, down_mine, down_away,
    local_sem, near_send, near_recv, pair_send, pair_recv, far_send, far_recv,
    up_send, up_recv, up_side_send, up_side_recv, slice_send, slice_recv,
    down_send, down_recv, down_side_send, down_side_recv,
    hid_send, hid_recv, sum_send, sum_recv,
):
    slots, rows, width = tok.shape[0], tok.shape[2], tok.shape[3]
    rows_up, rows_down = up_raw.shape[2], down_raw.shape[2]
    group = planes * 2 * rows_down
    groups = nz // (2 * planes)
    me, rank = lax.axis_index("dp"), lax.axis_index("tensor")
    z, x = me // 2, me % 2
    other = z * 2 + (1 - x)
    partner = [rank] + [flip(rank, 1 << bit) for bit in range(slots - 1)]
    others = [mask for mask in range(2, nz)] + [1]

    def plane(mask):
        return flip(z, mask) * 2 + x

    def remote(src, dst, send, recv, device):
        return pltpu.make_async_remote_copy(
            src_ref=src, dst_ref=dst, send_sem=send, recv_sem=recv,
            device_id=device, device_id_type=MESH,
        )

    def up_rows(at_z, at_x):
        return pl.ds(pl.multiple_of((at_z * 2 + at_x) * rows_up, rows_up), rows_up)

    def up_place(mask, at_x, c, slot):
        return up.at[slot, up_rows(flip(z, mask), at_x), c * group:(c + 1) * group]

    def up_source(mask, c, slot):
        parity = (z + mask) % 2
        first = pl.multiple_of((2 * c + parity) * group, group)
        return up_raw.at[0, slot, :, pl.ds(first, group)]

    def down_rows(at_z, at_x):
        row = (at_z // (2 * planes)) * group + ((at_z % planes) * 2 + at_x) * rows_down
        return pl.ds(pl.multiple_of(row, rows_down), rows_down)

    def gives_down(mask):
        if planes == 1:
            return mask % 2 == 0
        return (z + mask) % 2 == (z // planes) % 2

    def takes_down(mask):
        if planes == 1:
            return mask % 2 == 0
        return z % 2 == (flip(z, mask) // planes) % 2

    piece = rows // TOKEN_PIECES
    cut = rows // ROW_PIECES
    pieces = column_pieces(width)

    def near_copy(slot):
        return remote(tok_ref, tok.at[slot, 0], near_send.at[slot], near_recv.at[slot], (me, partner[slot]))

    def pair_copy(i):
        part = pl.ds(i * piece, piece)
        return remote(tok_ref.at[part], tok.at[0, 1, part], pair_send.at[i], pair_recv.at[i], (plane(1), rank))

    def far_copy(slot, i):
        part = pl.ds(i * piece, piece)
        return remote(
            tok.at[0, 1, part], tok.at[slot, 1, part], far_send.at[slot, i], far_recv.at[slot, i], (me, partner[slot])
        )

    def up_copy(mask, c, slot):
        at = c, mask, slot
        return remote(
            up_source(mask, c, slot), up_place(0, x, c, slot), up_send.at[at], up_recv.at[at], (plane(mask), rank)
        )

    def up_side(mask, c, slot):
        at = c, mask, slot
        place = up_place(mask, x, c, slot)
        src = up_source(0, c, slot) if mask == 0 else place
        return remote(src, place, up_side_send.at[at], up_side_recv.at[at], (other, rank))

    def slice_copy(slot):
        return remote(
            down_away.at[slot - 1], down_mine.at[slot], slice_send.at[slot], slice_recv.at[slot], (me, partner[slot])
        )

    def down_place(mask, at_x, q):
        first, wide = pieces[q]
        return down.at[:, down_rows(flip(z, mask), at_x), first:first + wide]

    def down_source(q):
        first, wide = pieces[q]
        return down_mine.at[:, :, first:first + wide]

    def down_copy(mask, q):
        return remote(
            down_source(q), down_place(0, x, q), down_send.at[mask, q], down_recv.at[mask, q], (plane(mask), rank)
        )

    def down_side(mask, q):
        src = down_source(q) if mask == 0 else down_place(mask, x, q)
        return remote(
            src, down_place(mask, x, q), down_side_send.at[mask, q], down_side_recv.at[mask, q], (other, rank)
        )

    def down_local(q):
        return pltpu.make_async_copy(down_source(q), down_place(0, x, q), local_sem.at[2 + q])

    def hid_copy(slot, c, far, i):
        part, columns = pl.ds(i * cut, cut), pl.ds(c * group, group)
        return remote(
            hid.at[0, far, part, columns], hid.at[slot, far, part, columns],
            hid_send.at[slot, c, far, i], hid_recv.at[slot, c, far, i], (me, partner[slot]),
        )

    def sum_copy(q):
        first, wide = pieces[q]
        columns = pl.ds(first, wide)
        return remote(stage.at[:, columns], landed.at[:, columns], sum_send.at[q], sum_recv.at[q], (plane(1), rank))


    def up_local(c, slot):
        return pltpu.make_async_copy(
            up_source(0, c, slot), up_place(0, x, c, slot), local_sem.at[2 + len(pieces) + c * slots + slot]
        )

    far_slots = range(slots - 1, 0, -1)

    fetch_down = pltpu.make_async_copy(down_raw.at[0], down_in, local_sem.at[0])
    fetch_tok = pltpu.make_async_copy(tok_ref, tok.at[0, 0], local_sem.at[1])
    fetch_down.start()
    fetch_tok.start()
    for c in range(groups):
        for slot in range(slots):
            up_local(c, slot).start()
    barrier = pltpu.get_barrier_semaphore()
    greeted = [(plane(mask), rank) for mask in range(1, nz)] + [(other, rank)]
    greeted += [(me, partner[slot]) for slot in range(1, slots)]
    for device in greeted:
        pl.semaphore_signal(barrier, inc=1, device_id=device, device_id_type=MESH)
    bits = [jnp.clip(bits_ref[slot, rank], 0, slots - 2) for slot in range(slots - 1)]
    fetch_down.wait()
    for bit in range(slots - 1):
        pick = jnp.int32(0)
        for slot in range(slots - 1):
            pick += jnp.where(bits[slot] == bit, slot + 1, 0)
        down_away[bit] = down_in[jnp.minimum(pick, slots - 1)]
    down_mine[0] = down_in[0]
    pl.semaphore_wait(barrier, len(greeted))

    def spread_down(q):
        for mask in others:
            when(gives_down(mask), lambda: down_copy(mask, q).start())

    def keep_down(q):
        def body():
            down_side(0, q).start()
            down_local(q).start()

        when(takes_down(0), body)

    def send_up(c, masks):
        for slot in range(slots):
            for mask in masks:
                up_copy(mask, c, slot).start()

    def keep_up(c):
        for slot in range(slots):
            up_side(0, c, slot).start()

    for slot in far_slots:
        slice_copy(slot).start()
    for slot in far_slots:
        near_copy(slot).start()
    send_up(0, others[:-1])
    for i in range(TOKEN_PIECES):
        pair_copy(i).start()
    send_up(0, others[-1:])
    keep_up(0)
    for c in range(1, groups):
        send_up(c, others)
        keep_up(c)

    def token_piece(i):
        pair_copy(i).wait_recv()
        for slot in far_slots:
            far_copy(slot, i).start()

    def up_arrived(mask, c, slot):
        place = up_place(mask, x, c, slot)
        at = c, mask, slot
        remote(place, place, up_send.at[at], up_recv.at[at], (plane(mask), rank)).wait_recv()
        up_side(mask, c, slot).start()

    def down_arrived(q):
        for mask in others:
            def body():
                place = down_place(mask, x, q)
                remote(
                    place, place, down_send.at[mask, q], down_recv.at[mask, q], (plane(mask), rank)
                ).wait_recv()
                down_side(mask, q).start()

            when(takes_down(mask), body)

    def down_complete(q):
        for mask in range(nz):
            def body():
                if mask == 0:
                    down_local(q).wait()
                place = down_place(mask, 1 - x, q)
                remote(
                    place, place, down_side_send.at[mask, q], down_side_recv.at[mask, q], (other, rank)
                ).wait_recv()

            when(takes_down(mask), body)

    def up_complete(c):
        for slot in range(slots):
            up_local(c, slot).wait()
            for mask in range(nz):
                place = up_place(mask, 1 - x, c, slot)
                at = c, mask, slot
                remote(place, place, up_side_send.at[at], up_side_recv.at[at], (other, rank)).wait_recv()

    def hidden(c, far):
        columns = slice(c * group, (c + 1) * group)
        for i in range(ROW_PIECES):
            part = slice(i * cut, (i + 1) * cut)
            pre = jnp.dot(tok[0, far, part], up[0, :, columns], preferred_element_type=jnp.float32)
            for slot in range(1, slots):
                pre += jnp.dot(
                    tok[1 + bits[slot - 1], far, part], up[slot, :, columns], preferred_element_type=jnp.float32
                )
            hid[0, far, part, columns] = jax.nn.gelu(pre, approximate=True).astype(hid.dtype)
            for slot in far_slots:
                hid_copy(slot, c, far, i).start()

    def slices_ready():
        for slot in range(1, slots):
            slice_copy(slot).wait_recv()

    def tokens_ready():
        fetch_tok.wait()
        for slot in far_slots:
            near_copy(slot).wait_recv()
            for i in range(TOKEN_PIECES):
                far_copy(slot, i).wait_recv()

    def forward_up(chunks, masks):
        for c in chunks:
            for slot in range(slots):
                for mask in masks:
                    up_arrived(mask, c, slot)

    def up_hidden(chunks, far):
        for c in chunks:
            if far:
                up_complete(c)
            hidden(c, far)

    at_end = jnp.logical_or(z == 0, z == nz - 1)
    begin, later = range(1), range(1, groups)

    def mixed(spread=False):
        @pl.when(at_end)
        def _():
            forward_up(later, others[:-1])
            forward_up(begin, others[-1:])

        @pl.when(jnp.logical_not(at_end))
        def _():
            forward_up(begin, others[-1:])
            if spread:
                for q in range(len(pieces)):
                    spread_down(q)
            forward_up(later, others[:-1])

    steps = {
        "far0": lambda: forward_up(begin, others[:-1]),
        "far1": lambda: forward_up(later, others[:-1]),
        "close0": lambda: forward_up(begin, others[-1:]),
        "close1": lambda: forward_up(later, others[-1:]),
        "all1": lambda: forward_up(later, others),
        "slices": slices_ready,
        "spread": lambda: [spread_down(q) for q in range(len(pieces))],
        "keep": lambda: [keep_down(q) for q in range(len(pieces))],
        "keep0": lambda: keep_down(0),
        "keep1": lambda: [keep_down(q) for q in range(1, len(pieces))],
        "spreadE": lambda: pl.when(at_end)(lambda: [spread_down(q) for q in range(len(pieces))] and None),
        "spreadM": lambda: pl.when(jnp.logical_not(at_end))(lambda: [spread_down(q) for q in range(len(pieces))] and None),
        "mixed": lambda: mixed(),
        "mixed_s": lambda: mixed(True),
        "spread0": lambda: spread_down(0),
        "spread1": lambda: [spread_down(q) for q in range(1, len(pieces))],
        "tok0": lambda: token_piece(0),
        "tok1": lambda: [token_piece(i) for i in range(1, TOKEN_PIECES)],
        "tokens": lambda: [token_piece(i) for i in range(TOKEN_PIECES)],
        "ready": tokens_ready,
        "hidden0": lambda: up_hidden(begin, 1),
        "hidden1": lambda: up_hidden(later, 1),
        "near": lambda: up_hidden(range(groups), 0),
        "near0": lambda: up_hidden(begin, 0),
        "near1": lambda: up_hidden(later, 0),
        "down0": lambda: down_arrived(0),
        "down1": lambda: down_arrived(1),
        "down2": lambda: down_arrived(2),
    }
    for step in ORDER:
        steps[step]()

    def product(far, part, columns):
        total = jnp.dot(hid[0, far, part], down[0, :, columns], preferred_element_type=jnp.float32)
        for slot in range(1, slots):
            total += jnp.dot(hid[slot, far, part], down[slot, :, columns], preferred_element_type=jnp.float32)
        return total

    def hid_arrived(far, i):
        for c in range(groups):
            for slot in far_slots:
                hid_copy(slot, c, far, i).wait_recv()

    for q, (first, wide) in enumerate(pieces):
        columns = slice(first, first + wide)
        if q == 0 and LATE_DOWN:
            down_arrived(1)
        if q == 1 and LATE_DOWN:
            down_arrived(2)
        down_complete(q)
        for i in range(ROW_PIECES):
            part = slice(i * cut, (i + 1) * cut)
            if q == 0:
                hid_arrived(1, i)
            stage[part, columns] = product(1, part, columns).astype(stage.dtype)
        sum_copy(q).start()
    for i in range(ROW_PIECES):
        part = slice(i * cut, (i + 1) * cut)
        hid_arrived(0, i)
        own_ref[part] = product(0, part, slice(None))
    for q in range(len(pieces)):
        sum_copy(q).wait_recv()

    for i in range(TOKEN_PIECES):
        pair_copy(i).wait_send()
    for slot in far_slots:
        near_copy(slot).wait_send()
        slice_copy(slot).wait_send()
        for i in range(TOKEN_PIECES):
            far_copy(slot, i).wait_send()
        for c in range(groups):
            for far in (1, 0):
                for i in range(ROW_PIECES):
                    hid_copy(slot, c, far, i).wait_send()
    for c in range(groups):
        for mask in range(nz):
            for slot in range(slots):
                if mask:
                    up_copy(mask, c, slot).wait_send()
                up_side(mask, c, slot).wait_send()
    for q in range(len(pieces)):
        for mask in range(nz):
            if mask:
                when(gives_down(mask), lambda: down_copy(mask, q).wait_send())
            when(takes_down(mask), lambda: down_side(mask, q).wait_send())
        sum_copy(q).wait_send()


def on_device(tokens, partner_bits, w_up, w_down):
    nz = lax.axis_size("dp") // 2
    slots = w_up.shape[1]
    rows, width = tokens.shape
    hidden = w_up.shape[3]
    rows_down = w_down.shape[2]
    half = hidden // 2
    planes = max(1, LANES // (2 * rows_down))
    groups = nz // (2 * planes)
    count = len(DOWN_SHARES)
    kind = tokens.dtype
    dma = pltpu.SemaphoreType.DMA
    own, landed = pl.pallas_call(
        functools.partial(kernel, nz, planes),
        out_shape=[pltpu.VMEM((rows, width), jnp.float32), pltpu.VMEM((rows, width), kind)],
        in_specs=[pl.BlockSpec(memory_space=pltpu.SMEM)] + [pl.BlockSpec(memory_space=pl.ANY)] * 3,
        out_specs=[pl.BlockSpec(memory_space=pltpu.VMEM)] * 2,
        scratch_shapes=[
            pltpu.VMEM((slots, 2, rows, width), kind),
            pltpu.VMEM((slots, width, half), kind),
            pltpu.VMEM((slots, half, width), kind),
            pltpu.VMEM((slots, 2, rows, half), kind),
            pltpu.VMEM((rows, width), kind),
            pltpu.VMEM(w_down.shape[1:], kind),
            pltpu.VMEM(w_down.shape[1:], kind),
            pltpu.VMEM((slots - 1,) + w_down.shape[2:], kind),
            dma((2 + count + groups * slots,)),
            dma((slots,)),
            dma((slots,)),
            dma((TOKEN_PIECES,)),
            dma((TOKEN_PIECES,)),
            dma((slots, TOKEN_PIECES)),
            dma((slots, TOKEN_PIECES)),
            dma((groups, nz, slots)),
            dma((groups, nz, slots)),
            dma((groups, nz, slots)),
            dma((groups, nz, slots)),
            dma((slots,)),
            dma((slots,)),
            dma((nz, count)),
            dma((nz, count)),
            dma((nz, count)),
            dma((nz, count)),
            dma((slots, groups, 2, ROW_PIECES)),
            dma((slots, groups, 2, ROW_PIECES)),
            dma((count,)),
            dma((count,)),
        ],
        compiler_params=pltpu.CompilerParams(
            collective_id=0, has_side_effects=True, vmem_limit_bytes=VMEM_BYTES
        ),
    )(partner_bits.T, tokens, w_up, w_down)
    return (own + landed.astype(jnp.float32)).astype(kind)


def solution(mesh):
    in_specs = (
        P("dp", "tensor"),
        P(),
        P("tensor", None, "dp", None),
        P("tensor", None, "dp", None),
    )
    return jax.shard_map(
        on_device, mesh=mesh, in_specs=in_specs, out_specs=P("dp", "tensor"), check_vma=False
    )
```

```python
import functools

import jax
import jax.numpy as jnp
from jax import lax
from jax.experimental import pallas as pl
from jax.experimental.pallas import tpu as pltpu
from jax.sharding import PartitionSpec as P

MESH = pl.DeviceIdType.MESH
LANES = 128
VMEM_BYTES = 65273856
TOKEN_PIECES = 1
ROW_PIECES = 2
ORDER = (
    "slices", "keep", "spreadE", "far0", "tokens", "spreadM", "mixed", "ready",
    "hidden0", "close1", "hidden1", "near0", "down0", "near1",
)
DOWN_SHARES = (2, 4, 4)


def flip(index, mask):
    bit = 1
    while bit <= mask:
        if mask & bit:
            index = index + (1 - 2 * ((index // bit) % 2)) * bit
        bit *= 2
    return index


def column_pieces(width):
    pieces, first = [], 0
    for share in DOWN_SHARES:
        pieces.append((first, width // share))
        first += width // share
    return pieces


def when(condition, body):
    if isinstance(condition, bool):
        if condition:
            body()
    else:
        pl.when(condition)(body)


def kernel(
    nz, planes, bits_ref, tok_ref, up_raw, down_raw, own_ref, landed,
    tok, up, down, hid, stage, down_in, down_mine, down_away,
    local_sem, near_send, near_recv, pair_send, pair_recv, far_send, far_recv,
    up_send, up_recv, up_side_send, up_side_recv, slice_send, slice_recv,
    down_send, down_recv, down_side_send, down_side_recv,
    hid_send, hid_recv, sum_send, sum_recv,
):
    slots, rows, width = tok.shape[0], tok.shape[2], tok.shape[3]
    rows_up, rows_down = up_raw.shape[2], down_raw.shape[2]
    group = planes * 2 * rows_down
    groups = nz // (2 * planes)
    me, rank = lax.axis_index("dp"), lax.axis_index("tensor")
    z, x = me // 2, me % 2
    other = z * 2 + (1 - x)
    partner = [rank] + [flip(rank, 1 << bit) for bit in range(slots - 1)]
    others = [mask for mask in range(2, nz)] + [1]

    def plane(mask):
        return flip(z, mask) * 2 + x

    def remote(src, dst, send, recv, device):
        return pltpu.make_async_remote_copy(
            src_ref=src, dst_ref=dst, send_sem=send, recv_sem=recv,
            device_id=device, device_id_type=MESH,
        )

    def up_rows(at_z, at_x):
        return pl.ds(pl.multiple_of((at_z * 2 + at_x) * rows_up, rows_up), rows_up)

    def up_place(mask, at_x, c, slot):
        return up.at[slot, up_rows(flip(z, mask), at_x), c * group:(c + 1) * group]

    def up_source(mask, c, slot):
        parity = (z + mask) % 2
        first = pl.multiple_of((2 * c + parity) * group, group)
        return up_raw.at[0, slot, :, pl.ds(first, group)]

    def down_rows(at_z, at_x):
        row = (at_z // (2 * planes)) * group + ((at_z % planes) * 2 + at_x) * rows_down
        return pl.ds(pl.multiple_of(row, rows_down), rows_down)

    def gives_down(mask):
        if planes == 1:
            return mask % 2 == 0
        return (z + mask) % 2 == (z // planes) % 2

    def takes_down(mask):
        if planes == 1:
            return mask % 2 == 0
        return z % 2 == (flip(z, mask) // planes) % 2

    piece = rows // TOKEN_PIECES
    cut = rows // ROW_PIECES
    pieces = column_pieces(width)

    def near_copy(slot):
        return remote(tok_ref, tok.at[slot, 0], near_send.at[slot], near_recv.at[slot], (me, partner[slot]))

    def pair_copy(i):
        part = pl.ds(i * piece, piece)
        return remote(tok_ref.at[part], tok.at[0, 1, part], pair_send.at[i], pair_recv.at[i], (plane(1), rank))

    def far_copy(slot, i):
        part = pl.ds(i * piece, piece)
        return remote(
            tok.at[0, 1, part], tok.at[slot, 1, part], far_send.at[slot, i], far_recv.at[slot, i], (me, partner[slot])
        )

    def up_copy(mask, c, slot):
        at = c, mask, slot
        return remote(
            up_source(mask, c, slot), up_place(0, x, c, slot), up_send.at[at], up_recv.at[at], (plane(mask), rank)
        )

    def up_side(mask, c, slot):
        at = c, mask, slot
        place = up_place(mask, x, c, slot)
        src = up_source(0, c, slot) if mask == 0 else place
        return remote(src, place, up_side_send.at[at], up_side_recv.at[at], (other, rank))

    def slice_copy(slot):
        return remote(
            down_away.at[slot - 1], down_mine.at[slot], slice_send.at[slot], slice_recv.at[slot], (me, partner[slot])
        )

    def down_place(mask, at_x, q):
        first, wide = pieces[q]
        return down.at[:, down_rows(flip(z, mask), at_x), first:first + wide]

    def down_source(q):
        first, wide = pieces[q]
        return down_mine.at[:, :, first:first + wide]

    def down_copy(mask, q):
        return remote(
            down_source(q), down_place(0, x, q), down_send.at[mask, q], down_recv.at[mask, q], (plane(mask), rank)
        )

    def down_side(mask, q):
        src = down_source(q) if mask == 0 else down_place(mask, x, q)
        return remote(
            src, down_place(mask, x, q), down_side_send.at[mask, q], down_side_recv.at[mask, q], (other, rank)
        )

    def down_local(q):
        return pltpu.make_async_copy(down_source(q), down_place(0, x, q), local_sem.at[2 + q])

    def hid_copy(slot, c, far, i):
        part, columns = pl.ds(i * cut, cut), pl.ds(c * group, group)
        return remote(
            hid.at[0, far, part, columns], hid.at[slot, far, part, columns],
            hid_send.at[slot, c, far, i], hid_recv.at[slot, c, far, i], (me, partner[slot]),
        )

    def sum_copy(q):
        first, wide = pieces[q]
        columns = pl.ds(first, wide)
        return remote(stage.at[:, columns], landed.at[:, columns], sum_send.at[q], sum_recv.at[q], (plane(1), rank))


    def up_local(c, slot):
        return pltpu.make_async_copy(
            up_source(0, c, slot), up_place(0, x, c, slot), local_sem.at[2 + len(pieces) + c * slots + slot]
        )

    far_slots = range(slots - 1, 0, -1)

    fetch_down = pltpu.make_async_copy(down_raw.at[0], down_in, local_sem.at[0])
    fetch_tok = pltpu.make_async_copy(tok_ref, tok.at[0, 0], local_sem.at[1])
    fetch_down.start()
    fetch_tok.start()
    for c in range(groups):
        for slot in range(slots):
            up_local(c, slot).start()
    barrier = pltpu.get_barrier_semaphore()
    greeted = [(plane(mask), rank) for mask in range(1, nz)] + [(other, rank)]
    greeted += [(me, partner[slot]) for slot in range(1, slots)]
    for device in greeted:
        pl.semaphore_signal(barrier, inc=1, device_id=device, device_id_type=MESH)
    bits = [jnp.clip(bits_ref[slot, rank], 0, slots - 2) for slot in range(slots - 1)]
    fetch_down.wait()
    for bit in range(slots - 1):
        pick = jnp.int32(0)
        for slot in range(slots - 1):
            pick += jnp.where(bits[slot] == bit, slot + 1, 0)
        down_away[bit] = down_in[jnp.minimum(pick, slots - 1)]
    down_mine[0] = down_in[0]
    pl.semaphore_wait(barrier, len(greeted))

    def spread_down(q):
        for mask in others:
            when(gives_down(mask), lambda: down_copy(mask, q).start())

    def keep_down(q):
        def body():
            down_side(0, q).start()
            down_local(q).start()

        when(takes_down(0), body)

    def send_up(c, masks):
        for slot in range(slots):
            for mask in masks:
                up_copy(mask, c, slot).start()

    def keep_up(c):
        for slot in range(slots):
            up_side(0, c, slot).start()

    send_up(0, others[:-1])
    for slot in far_slots:
        slice_copy(slot).start()
    for slot in far_slots:
        near_copy(slot).start()
    for i in range(TOKEN_PIECES):
        pair_copy(i).start()
    send_up(0, others[-1:])
    keep_up(0)
    for c in range(1, groups):
        send_up(c, others)
        keep_up(c)

    def token_piece(i):
        pair_copy(i).wait_recv()
        for slot in far_slots:
            far_copy(slot, i).start()

    def up_arrived(mask, c, slot):
        place = up_place(mask, x, c, slot)
        at = c, mask, slot
        remote(place, place, up_send.at[at], up_recv.at[at], (plane(mask), rank)).wait_recv()
        up_side(mask, c, slot).start()

    def down_arrived(q):
        for mask in others:
            def body():
                place = down_place(mask, x, q)
                remote(
                    place, place, down_send.at[mask, q], down_recv.at[mask, q], (plane(mask), rank)
                ).wait_recv()
                down_side(mask, q).start()

            when(takes_down(mask), body)

    def down_complete(q):
        for mask in range(nz):
            def body():
                if mask == 0:
                    down_local(q).wait()
                place = down_place(mask, 1 - x, q)
                remote(
                    place, place, down_side_send.at[mask, q], down_side_recv.at[mask, q], (other, rank)
                ).wait_recv()

            when(takes_down(mask), body)

    def up_complete(c):
        for slot in range(slots):
            up_local(c, slot).wait()
            for mask in range(nz):
                place = up_place(mask, 1 - x, c, slot)
                at = c, mask, slot
                remote(place, place, up_side_send.at[at], up_side_recv.at[at], (other, rank)).wait_recv()

    def hidden(c, far):
        columns = slice(c * group, (c + 1) * group)
        for i in range(ROW_PIECES):
            part = slice(i * cut, (i + 1) * cut)
            pre = jnp.dot(tok[0, far, part], up[0, :, columns], preferred_element_type=jnp.float32)
            for slot in range(1, slots):
                pre += jnp.dot(
                    tok[1 + bits[slot - 1], far, part], up[slot, :, columns], preferred_element_type=jnp.float32
                )
            hid[0, far, part, columns] = jax.nn.gelu(pre, approximate=True).astype(hid.dtype)
            for slot in far_slots:
                hid_copy(slot, c, far, i).start()

    def slices_ready():
        for slot in range(1, slots):
            slice_copy(slot).wait_recv()

    def tokens_ready():
        fetch_tok.wait()
        for slot in far_slots:
            near_copy(slot).wait_recv()
            for i in range(TOKEN_PIECES):
                far_copy(slot, i).wait_recv()

    def forward_up(chunks, masks):
        for c in chunks:
            for slot in range(slots):
                for mask in masks:
                    up_arrived(mask, c, slot)

    def up_hidden(chunks, far):
        for c in chunks:
            if far:
                up_complete(c)
            hidden(c, far)

    at_end = jnp.logical_or(z == 0, z == nz - 1)
    begin, later = range(1), range(1, groups)

    def spread_all():
        for q in range(len(pieces)):
            spread_down(q)

    def mixed():
        @pl.when(at_end)
        def _():
            forward_up(later, others[:-1])
            forward_up(begin, others[-1:])

        @pl.when(jnp.logical_not(at_end))
        def _():
            forward_up(begin, others[-1:])
            forward_up(later, others[:-1])

    steps = {
        "slices": slices_ready,
        "keep": lambda: [keep_down(q) for q in range(len(pieces))],
        "far0": lambda: forward_up(begin, others[:-1]),
        "spreadE": lambda: pl.when(at_end)(spread_all),
        "tokens": lambda: [token_piece(i) for i in range(TOKEN_PIECES)],
        "spreadM": lambda: pl.when(jnp.logical_not(at_end))(spread_all),
        "mixed": mixed,
        "ready": tokens_ready,
        "hidden0": lambda: up_hidden(begin, 1),
        "close1": lambda: forward_up(later, others[-1:]),
        "hidden1": lambda: up_hidden(later, 1),
        "near0": lambda: up_hidden(begin, 0),
        "down0": lambda: down_arrived(0),
        "near1": lambda: up_hidden(later, 0),
    }
    for step in ORDER:
        steps[step]()

    def product(far, part, columns):
        total = jnp.dot(hid[0, far, part], down[0, :, columns], preferred_element_type=jnp.float32)
        for slot in range(1, slots):
            total += jnp.dot(hid[slot, far, part], down[slot, :, columns], preferred_element_type=jnp.float32)
        return total

    def hid_arrived(far, i):
        for c in range(groups):
            for slot in far_slots:
                hid_copy(slot, c, far, i).wait_recv()

    for q, (first, wide) in enumerate(pieces):
        columns = slice(first, first + wide)
        if q + 1 < len(pieces):
            down_arrived(q + 1)
        down_complete(q)
        for i in range(ROW_PIECES):
            part = slice(i * cut, (i + 1) * cut)
            if q == 0:
                hid_arrived(1, i)
            stage[part, columns] = product(1, part, columns).astype(stage.dtype)
        sum_copy(q).start()
    for i in range(ROW_PIECES):
        part = slice(i * cut, (i + 1) * cut)
        hid_arrived(0, i)
        own_ref[part] = product(0, part, slice(None))
    for q in range(len(pieces)):
        sum_copy(q).wait_recv()

    for i in range(TOKEN_PIECES):
        pair_copy(i).wait_send()
    for slot in far_slots:
        near_copy(slot).wait_send()
        slice_copy(slot).wait_send()
        for i in range(TOKEN_PIECES):
            far_copy(slot, i).wait_send()
        for c in range(groups):
            for far in (1, 0):
                for i in range(ROW_PIECES):
                    hid_copy(slot, c, far, i).wait_send()
    for c in range(groups):
        for mask in range(nz):
            for slot in range(slots):
                if mask:
                    up_copy(mask, c, slot).wait_send()
                up_side(mask, c, slot).wait_send()
    for q in range(len(pieces)):
        for mask in range(nz):
            if mask:
                when(gives_down(mask), lambda: down_copy(mask, q).wait_send())
            when(takes_down(mask), lambda: down_side(mask, q).wait_send())
        sum_copy(q).wait_send()


def on_device(tokens, partner_bits, w_up, w_down):
    nz = lax.axis_size("dp") // 2
    slots = w_up.shape[1]
    rows, width = tokens.shape
    hidden = w_up.shape[3]
    rows_down = w_down.shape[2]
    half = hidden // 2
    planes = max(1, LANES // (2 * rows_down))
    groups = nz // (2 * planes)
    count = len(DOWN_SHARES)
    kind = tokens.dtype
    dma = pltpu.SemaphoreType.DMA
    own, landed = pl.pallas_call(
        functools.partial(kernel, nz, planes),
        out_shape=[pltpu.VMEM((rows, width), jnp.float32), pltpu.VMEM((rows, width), kind)],
        in_specs=[pl.BlockSpec(memory_space=pltpu.SMEM)] + [pl.BlockSpec(memory_space=pl.ANY)] * 3,
        out_specs=[pl.BlockSpec(memory_space=pltpu.VMEM)] * 2,
        scratch_shapes=[
            pltpu.VMEM((slots, 2, rows, width), kind),
            pltpu.VMEM((slots, width, half), kind),
            pltpu.VMEM((slots, half, width), kind),
            pltpu.VMEM((slots, 2, rows, half), kind),
            pltpu.VMEM((rows, width), kind),
            pltpu.VMEM(w_down.shape[1:], kind),
            pltpu.VMEM(w_down.shape[1:], kind),
            pltpu.VMEM((slots - 1,) + w_down.shape[2:], kind),
            dma((2 + count + groups * slots,)),
            dma((slots,)),
            dma((slots,)),
            dma((TOKEN_PIECES,)),
            dma((TOKEN_PIECES,)),
            dma((slots, TOKEN_PIECES)),
            dma((slots, TOKEN_PIECES)),
            dma((groups, nz, slots)),
            dma((groups, nz, slots)),
            dma((groups, nz, slots)),
            dma((groups, nz, slots)),
            dma((slots,)),
            dma((slots,)),
            dma((nz, count)),
            dma((nz, count)),
            dma((nz, count)),
            dma((nz, count)),
            dma((slots, groups, 2, ROW_PIECES)),
            dma((slots, groups, 2, ROW_PIECES)),
            dma((count,)),
            dma((count,)),
        ],
        compiler_params=pltpu.CompilerParams(
            collective_id=0, has_side_effects=True, vmem_limit_bytes=VMEM_BYTES
        ),
    )(partner_bits.T, tokens, w_up, w_down)
    return (own + landed.astype(jnp.float32)).astype(kind)


def solution(mesh):
    in_specs = (
        P("dp", "tensor"),
        P(),
        P("tensor", None, "dp", None),
        P("tensor", None, "dp", None),
    )
    return jax.shard_map(
        on_device, mesh=mesh, in_specs=in_specs, out_specs=P("dp", "tensor"), check_vma=False
    )
```

```python
import functools

import jax
import jax.numpy as jnp
from jax import lax
from jax.experimental import pallas as pl
from jax.experimental.pallas import tpu as pltpu
from jax.sharding import PartitionSpec as P

MESH = pl.DeviceIdType.MESH
LANES = 128
VMEM_BYTES = 65273856
TOKEN_PIECES = 1
ROW_PIECES = 2
ORDER = (
    "slices", "keep", "spreadE", "far0", "tokens", "spreadM", "mixed", "ready",
    "hidden0", "close1", "hidden1", "down0", "near0", "near1",
)
DOWN_SHARES = (2, 2)


def flip(index, mask):
    bit = 1
    while bit <= mask:
        if mask & bit:
            index = index + (1 - 2 * ((index // bit) % 2)) * bit
        bit *= 2
    return index


def column_pieces(width):
    pieces, first = [], 0
    for share in DOWN_SHARES:
        pieces.append((first, width // share))
        first += width // share
    return pieces


def when(condition, body):
    if isinstance(condition, bool):
        if condition:
            body()
    else:
        pl.when(condition)(body)


def kernel(
    nz, planes, bits_ref, tok_ref, up_raw, down_raw, own_ref, landed,
    tok, up, down, hid, stage, down_in, down_mine, down_away,
    local_sem, near_send, near_recv, pair_send, pair_recv, far_send, far_recv,
    up_send, up_recv, up_side_send, up_side_recv, slice_send, slice_recv,
    down_send, down_recv, down_side_send, down_side_recv,
    hid_send, hid_recv, sum_send, sum_recv,
):
    slots, rows, width = tok.shape[0], tok.shape[2], tok.shape[3]
    rows_up, rows_down = up_raw.shape[2], down_raw.shape[2]
    group = planes * 2 * rows_down
    groups = nz // (2 * planes)
    me, rank = lax.axis_index("dp"), lax.axis_index("tensor")
    z, x = me // 2, me % 2
    other = z * 2 + (1 - x)
    partner = [rank] + [flip(rank, 1 << bit) for bit in range(slots - 1)]
    others = [mask for mask in range(2, nz)] + [1]

    def plane(mask):
        return flip(z, mask) * 2 + x

    def remote(src, dst, send, recv, device):
        return pltpu.make_async_remote_copy(
            src_ref=src, dst_ref=dst, send_sem=send, recv_sem=recv,
            device_id=device, device_id_type=MESH,
        )

    def up_rows(at_z, at_x):
        return pl.ds(pl.multiple_of((at_z * 2 + at_x) * rows_up, rows_up), rows_up)

    def up_place(mask, at_x, c, slot):
        return up.at[slot, up_rows(flip(z, mask), at_x), c * group:(c + 1) * group]

    def up_source(mask, c, slot):
        parity = (z + mask) % 2
        first = pl.multiple_of((2 * c + parity) * group, group)
        return up_raw.at[0, slot, :, pl.ds(first, group)]

    def down_rows(at_z, at_x):
        row = (at_z // (2 * planes)) * group + ((at_z % planes) * 2 + at_x) * rows_down
        return pl.ds(pl.multiple_of(row, rows_down), rows_down)

    def gives_down(mask):
        if planes == 1:
            return mask % 2 == 0
        return (z + mask) % 2 == (z // planes) % 2

    def takes_down(mask):
        if planes == 1:
            return mask % 2 == 0
        return z % 2 == (flip(z, mask) // planes) % 2

    piece = rows // TOKEN_PIECES
    cut = rows // ROW_PIECES
    pieces = column_pieces(width)

    def near_copy(slot):
        return remote(tok_ref, tok.at[slot, 0], near_send.at[slot], near_recv.at[slot], (me, partner[slot]))

    def pair_copy(i):
        part = pl.ds(i * piece, piece)
        return remote(tok_ref.at[part], tok.at[0, 1, part], pair_send.at[i], pair_recv.at[i], (plane(1), rank))

    def far_copy(slot, i):
        part = pl.ds(i * piece, piece)
        return remote(
            tok.at[0, 1, part], tok.at[slot, 1, part], far_send.at[slot, i], far_recv.at[slot, i], (me, partner[slot])
        )

    def up_copy(mask, c, slot):
        at = c, mask, slot
        return remote(
            up_source(mask, c, slot), up_place(0, x, c, slot), up_send.at[at], up_recv.at[at], (plane(mask), rank)
        )

    def up_side(mask, c, slot):
        at = c, mask, slot
        place = up_place(mask, x, c, slot)
        src = up_source(0, c, slot) if mask == 0 else place
        return remote(src, place, up_side_send.at[at], up_side_recv.at[at], (other, rank))

    def slice_copy(slot):
        return remote(
            down_away.at[slot - 1], down_mine.at[slot], slice_send.at[slot], slice_recv.at[slot], (me, partner[slot])
        )

    def down_place(mask, at_x, q, slot):
        first, wide = pieces[q]
        return down.at[slot, down_rows(flip(z, mask), at_x), first:first + wide]

    def down_source(q, slot):
        first, wide = pieces[q]
        return down_mine.at[slot, :, first:first + wide]

    def down_copy(mask, q, slot):
        at = mask, q, slot
        return remote(
            down_source(q, slot), down_place(0, x, q, slot), down_send.at[at], down_recv.at[at], (plane(mask), rank)
        )

    def down_side(mask, q, slot):
        at = mask, q, slot
        place = down_place(mask, x, q, slot)
        src = down_source(q, slot) if mask == 0 else place
        return remote(src, place, down_side_send.at[at], down_side_recv.at[at], (other, rank))

    def down_local(q, slot):
        return pltpu.make_async_copy(
            down_source(q, slot), down_place(0, x, q, slot), local_sem.at[2 + q * slots + slot]
        )

    def hid_copy(slot, c, far, i):
        part, columns = pl.ds(i * cut, cut), pl.ds(c * group, group)
        return remote(
            hid.at[0, far, part, columns], hid.at[slot, far, part, columns],
            hid_send.at[slot, c, far, i], hid_recv.at[slot, c, far, i], (me, partner[slot]),
        )

    def sum_copy(q):
        first, wide = pieces[q]
        columns = pl.ds(first, wide)
        return remote(stage.at[:, columns], landed.at[:, columns], sum_send.at[q], sum_recv.at[q], (plane(1), rank))


    def up_local(c, slot):
        return pltpu.make_async_copy(
            up_source(0, c, slot), up_place(0, x, c, slot), local_sem.at[2 + (len(pieces) + c) * slots + slot]
        )

    far_slots = range(slots - 1, 0, -1)

    fetch_down = pltpu.make_async_copy(down_raw.at[0], down_in, local_sem.at[0])
    fetch_tok = pltpu.make_async_copy(tok_ref, tok.at[0, 0], local_sem.at[1])
    fetch_down.start()
    fetch_tok.start()
    for c in range(groups):
        for slot in range(slots):
            up_local(c, slot).start()
    barrier = pltpu.get_barrier_semaphore()
    greeted = [(plane(mask), rank) for mask in range(1, nz)] + [(other, rank)]
    greeted += [(me, partner[slot]) for slot in range(1, slots)]
    for device in greeted:
        pl.semaphore_signal(barrier, inc=1, device_id=device, device_id_type=MESH)
    bits = [jnp.clip(bits_ref[slot, rank], 0, slots - 2) for slot in range(slots - 1)]
    fetch_down.wait()
    for bit in range(slots - 1):
        pick = jnp.int32(0)
        for slot in range(slots - 1):
            pick += jnp.where(bits[slot] == bit, slot + 1, 0)
        down_away[bit] = down_in[jnp.minimum(pick, slots - 1)]
    down_mine[0] = down_in[0]
    pl.semaphore_wait(barrier, len(greeted))

    def spread_down(q):
        for slot in range(slots):
            for mask in others:
                when(gives_down(mask), lambda: down_copy(mask, q, slot).start())

    def keep_down(q):
        def body():
            for slot in range(slots):
                down_side(0, q, slot).start()
                down_local(q, slot).start()

        when(takes_down(0), body)

    def send_up(c, masks):
        for slot in range(slots):
            for mask in masks:
                up_copy(mask, c, slot).start()

    def keep_up(c):
        for slot in range(slots):
            up_side(0, c, slot).start()

    send_up(0, others[:-1])
    for slot in far_slots:
        slice_copy(slot).start()
    for slot in far_slots:
        near_copy(slot).start()
    for i in range(TOKEN_PIECES):
        pair_copy(i).start()
    send_up(0, others[-1:])
    keep_up(0)
    for c in range(1, groups):
        send_up(c, others)
        keep_up(c)

    def token_piece(i):
        pair_copy(i).wait_recv()
        for slot in far_slots:
            far_copy(slot, i).start()

    def up_arrived(mask, c, slot):
        place = up_place(mask, x, c, slot)
        at = c, mask, slot
        remote(place, place, up_send.at[at], up_recv.at[at], (plane(mask), rank)).wait_recv()
        up_side(mask, c, slot).start()

    def down_arrived(q):
        for slot in range(slots):
            for mask in others:
                def body():
                    at = mask, q, slot
                    place = down_place(mask, x, q, slot)
                    remote(place, place, down_send.at[at], down_recv.at[at], (plane(mask), rank)).wait_recv()
                    down_side(mask, q, slot).start()

                when(takes_down(mask), body)

    def down_complete(q):
        for slot in range(slots):
            for mask in range(nz):
                def body():
                    if mask == 0:
                        down_local(q, slot).wait()
                    at = mask, q, slot
                    place = down_place(mask, 1 - x, q, slot)
                    remote(place, place, down_side_send.at[at], down_side_recv.at[at], (other, rank)).wait_recv()

                when(takes_down(mask), body)

    def up_complete(c):
        for slot in range(slots):
            up_local(c, slot).wait()
            for mask in range(nz):
                place = up_place(mask, 1 - x, c, slot)
                at = c, mask, slot
                remote(place, place, up_side_send.at[at], up_side_recv.at[at], (other, rank)).wait_recv()

    def hidden(c, far):
        columns = slice(c * group, (c + 1) * group)
        for i in range(ROW_PIECES):
            part = slice(i * cut, (i + 1) * cut)
            pre = jnp.dot(tok[0, far, part], up[0, :, columns], preferred_element_type=jnp.float32)
            for slot in range(1, slots):
                pre += jnp.dot(
                    tok[1 + bits[slot - 1], far, part], up[slot, :, columns], preferred_element_type=jnp.float32
                )
            hid[0, far, part, columns] = jax.nn.gelu(pre, approximate=True).astype(hid.dtype)
            for slot in far_slots:
                hid_copy(slot, c, far, i).start()

    def slices_ready():
        for slot in range(1, slots):
            slice_copy(slot).wait_recv()

    def tokens_ready():
        fetch_tok.wait()
        for slot in far_slots:
            near_copy(slot).wait_recv()
            for i in range(TOKEN_PIECES):
                far_copy(slot, i).wait_recv()

    def forward_up(chunks, masks):
        for c in chunks:
            for slot in range(slots):
                for mask in masks:
                    up_arrived(mask, c, slot)

    def up_hidden(chunks, far):
        for c in chunks:
            if far:
                up_complete(c)
            hidden(c, far)

    at_end = jnp.logical_or(z == 0, z == nz - 1)
    begin, later = range(1), range(1, groups)

    def spread_all():
        for q in range(len(pieces)):
            spread_down(q)

    def mixed():
        @pl.when(at_end)
        def _():
            forward_up(later, others[:-1])
            forward_up(begin, others[-1:])

        @pl.when(jnp.logical_not(at_end))
        def _():
            forward_up(begin, others[-1:])
            forward_up(later, others[:-1])

    steps = {
        "slices": slices_ready,
        "keep": lambda: [keep_down(q) for q in range(len(pieces))],
        "far0": lambda: forward_up(begin, others[:-1]),
        "spreadE": lambda: pl.when(at_end)(spread_all),
        "tokens": lambda: [token_piece(i) for i in range(TOKEN_PIECES)],
        "spreadM": lambda: pl.when(jnp.logical_not(at_end))(spread_all),
        "mixed": mixed,
        "ready": tokens_ready,
        "hidden0": lambda: up_hidden(begin, 1),
        "close1": lambda: forward_up(later, others[-1:]),
        "hidden1": lambda: up_hidden(later, 1),
        "near0": lambda: up_hidden(begin, 0),
        "down0": lambda: down_arrived(0),
        "near1": lambda: up_hidden(later, 0),
    }
    for step in ORDER:
        steps[step]()

    def product(far, part, columns):
        total = jnp.dot(hid[0, far, part], down[0, :, columns], preferred_element_type=jnp.float32)
        for slot in range(1, slots):
            total += jnp.dot(hid[slot, far, part], down[slot, :, columns], preferred_element_type=jnp.float32)
        return total

    def hid_arrived(far, i):
        for c in range(groups):
            for slot in far_slots:
                hid_copy(slot, c, far, i).wait_recv()

    for q, (first, wide) in enumerate(pieces):
        columns = slice(first, first + wide)
        if q + 1 < len(pieces):
            down_arrived(q + 1)
        down_complete(q)
        for i in range(ROW_PIECES):
            part = slice(i * cut, (i + 1) * cut)
            if q == 0:
                hid_arrived(1, i)
            stage[part, columns] = product(1, part, columns).astype(stage.dtype)
        sum_copy(q).start()
    for i in range(ROW_PIECES):
        part = slice(i * cut, (i + 1) * cut)
        hid_arrived(0, i)
        own_ref[part] = product(0, part, slice(None))
    for q in range(len(pieces)):
        sum_copy(q).wait_recv()

    for i in range(TOKEN_PIECES):
        pair_copy(i).wait_send()
    for slot in far_slots:
        near_copy(slot).wait_send()
        slice_copy(slot).wait_send()
        for i in range(TOKEN_PIECES):
            far_copy(slot, i).wait_send()
        for c in range(groups):
            for far in (1, 0):
                for i in range(ROW_PIECES):
                    hid_copy(slot, c, far, i).wait_send()
    for c in range(groups):
        for mask in range(nz):
            for slot in range(slots):
                if mask:
                    up_copy(mask, c, slot).wait_send()
                up_side(mask, c, slot).wait_send()
    for q in range(len(pieces)):
        for slot in range(slots):
            for mask in range(nz):
                if mask:
                    when(gives_down(mask), lambda: down_copy(mask, q, slot).wait_send())
                when(takes_down(mask), lambda: down_side(mask, q, slot).wait_send())
        sum_copy(q).wait_send()


def on_device(tokens, partner_bits, w_up, w_down):
    nz = lax.axis_size("dp") // 2
    slots = w_up.shape[1]
    rows, width = tokens.shape
    hidden = w_up.shape[3]
    rows_down = w_down.shape[2]
    half = hidden // 2
    planes = max(1, LANES // (2 * rows_down))
    groups = nz // (2 * planes)
    count = len(DOWN_SHARES)
    kind = tokens.dtype
    dma = pltpu.SemaphoreType.DMA
    own, landed = pl.pallas_call(
        functools.partial(kernel, nz, planes),
        out_shape=[pltpu.VMEM((rows, width), jnp.float32), pltpu.VMEM((rows, width), kind)],
        in_specs=[pl.BlockSpec(memory_space=pltpu.SMEM)] + [pl.BlockSpec(memory_space=pl.ANY)] * 3,
        out_specs=[pl.BlockSpec(memory_space=pltpu.VMEM)] * 2,
        scratch_shapes=[
            pltpu.VMEM((slots, 2, rows, width), kind),
            pltpu.VMEM((slots, width, half), kind),
            pltpu.VMEM((slots, half, width), kind),
            pltpu.VMEM((slots, 2, rows, half), kind),
            pltpu.VMEM((rows, width), kind),
            pltpu.VMEM(w_down.shape[1:], kind),
            pltpu.VMEM(w_down.shape[1:], kind),
            pltpu.VMEM((slots - 1,) + w_down.shape[2:], kind),
            dma((2 + (count + groups) * slots,)),
            dma((slots,)),
            dma((slots,)),
            dma((TOKEN_PIECES,)),
            dma((TOKEN_PIECES,)),
            dma((slots, TOKEN_PIECES)),
            dma((slots, TOKEN_PIECES)),
            dma((groups, nz, slots)),
            dma((groups, nz, slots)),
            dma((groups, nz, slots)),
            dma((groups, nz, slots)),
            dma((slots,)),
            dma((slots,)),
            dma((nz, count, slots)),
            dma((nz, count, slots)),
            dma((nz, count, slots)),
            dma((nz, count, slots)),
            dma((slots, groups, 2, ROW_PIECES)),
            dma((slots, groups, 2, ROW_PIECES)),
            dma((count,)),
            dma((count,)),
        ],
        compiler_params=pltpu.CompilerParams(
            collective_id=0, has_side_effects=True, vmem_limit_bytes=VMEM_BYTES
        ),
    )(partner_bits.T, tokens, w_up, w_down)
    return (own + landed.astype(jnp.float32)).astype(kind)


def solution(mesh):
    in_specs = (
        P("dp", "tensor"),
        P(),
        P("tensor", None, "dp", None),
        P("tensor", None, "dp", None),
    )
    return jax.shard_map(
        on_device, mesh=mesh, in_specs=in_specs, out_specs=P("dp", "tensor"), check_vma=False
    )
```
